32 devices in a mesh: led: 8 (over y, x, core), tile: 4 (over z).
Axes of the slice: x: 2, y: 2, z: 4, core: 2. Of those that a mesh axis runs over, the one named last changes fastest.
Arguments:
- spectrum: bfloat16 [1024, 2048], replicated, may hold values from -6 to 6
- pupils: bfloat16 [4, 512, 1024], replicated, may hold values from -1.5 to 1.5
- offsets: int32 [32, 2], P(('led', 'tile')), may hold values from 0 to 512
- measured: bfloat16 [32, 512, 512], P(('led', 'tile')), may hold values from 0.099609375 to 4
Outputs:
- spectrum_grad: float32 [4, 256, 2048], P('tile', 'led')
- pupil_grad: float32 [4, 512, 1024], P(None, 'led')
The draws below stay inside these ranges and needn't reach their ends.
Inputs may be any that keep to these rules, and one draw needn't show every extreme that they name: `offsets`: each patch lies inside the spectrum.
All inputs are finite; a program needn't handle non-finite values.
Results may differ from the reference program's by a relative error of at most 0.011.
Values sent between devices are 32-bit elements; how exact they have to be, the bound alone decides.
No kernel may reach another device: no remote copies, remote signals or barrier semaphores. Data moves between devices by JAX's collectives and lax.ppermute only.
A program may use at most 128 MiB of HBM per device.

```python
import math
import jax
import jax.numpy as jnp
from jax import lax

PATCH = 512
MODES = 4
LEDS = 32
STRIP = 256
SPEC = 1024
N_TILE = 4


def touch_ends(values, own_key, low, largest):
    index_at = [jax.random.randint(jax.random.fold_in(own_key, axis), (), 0, length) for axis, length in enumerate(values.shape)]
    main_axis = values.shape.index(max(values.shape))
    beside = index_at[:main_axis] + [(index_at[main_axis] + 1) % values.shape[main_axis]] + index_at[main_axis + 1:]
    return values.at[tuple(index_at)].set(low).at[tuple(beside)].set(largest)


def block_levels(rng, dims, shards, smallest, top_value):
    loudness, own = 1.0, jax.random.fold_in(rng, 6)
    for position, blocks in shards:
        heights = jnp.exp(jax.random.uniform(jax.random.fold_in(own, position), (blocks,), jnp.float32, smallest / len(shards), top_value / len(shards)))
        loudness = loudness * jnp.repeat(heights, dims[position] // blocks).reshape([-1 if axis == position else 1 for axis in range(len(dims))])
    return loudness


def bell_draw(own_key, shape, spread, most, held_as=jnp.bfloat16):
    drawn = jax.random.normal(own_key, shape, jnp.float32) * spread
    return jnp.minimum(jnp.maximum(drawn, -most), most).astype(held_as)


def setup_inputs(seed: int = 0) -> dict:
    seeds = jax.random.split(jax.random.key(seed), 5)
    spectrum = bell_draw(seeds[0], (SPEC, 2 * SPEC), 1.0, 6.0)
    pupils = bell_draw(seeds[1], (MODES, PATCH, 2 * PATCH), 0.25, 1.5)
    offsets = touch_ends(jax.random.randint(seeds[2], (LEDS, 2), 0, SPEC - PATCH + 1), jax.random.fold_in(seeds[2], 1), 0, SPEC - PATCH).astype(jnp.int32)
    measured = jnp.clip(jnp.exp(math.log(4.0) - 3.6927934 * jax.random.uniform(seeds[3], (LEDS, PATCH, PATCH), jnp.float32) ** block_levels(seeds[3], (LEDS, PATCH, PATCH), ((0, 32),), -0.2, 0.2)), 0.099609375, 4.0).astype(jnp.bfloat16)
    return dict(spectrum=spectrum, pupils=pupils, offsets=offsets, measured=measured)


def dft_tables(length):
    positions = jnp.arange(length, dtype=jnp.int32)
    angles = (positions[:, None] * positions[None, :] % length).astype(jnp.float32) * (2.0 * math.pi / length)
    factor = 1.0 / math.sqrt(length)
    return ((jnp.cos(angles) * factor).astype(jnp.bfloat16), (jnp.sin(angles) * factor).astype(jnp.bfloat16))

def product(form, left, right):
    return jnp.einsum(form, left.astype(jnp.float32), right.astype(jnp.float32), precision=lax.Precision.HIGHEST)

def emitter_model(patch_real, patch_imaginary, pupils, intensity_measurement, cosine_lookup, sine_lookup):
    length = patch_real.shape[0]
    pupil_re = pupils[:, :, :length].astype(jnp.float32)
    pupil_im = pupils[:, :, length:].astype(jnp.float32)
    real_part = patch_real.astype(jnp.float32)[None]
    imag_part = patch_imaginary.astype(jnp.float32)[None]
    exit_field = jnp.concatenate([real_part * pupil_re - imag_part * pupil_im, real_part * pupil_im + imag_part * pupil_re], axis=2).astype(jnp.bfloat16)
    cos_rows = product('jk,mkc->mjc', cosine_lookup, exit_field)
    sin_rows = product('jk,mkc->mjc', sine_lookup, exit_field)
    half_re = cos_rows[:, :, :length] - sin_rows[:, :, length:]
    half_im = cos_rows[:, :, length:] + sin_rows[:, :, :length]
    stacked = jnp.concatenate([half_re, half_im], axis=1).astype(jnp.bfloat16)
    cos_cols = product('mjk,kl->mjl', stacked, cosine_lookup)
    sin_cols = product('mjk,kl->mjl', stacked, sine_lookup)
    field_re = cos_cols[:, :length] - sin_cols[:, length:]
    field_im = cos_cols[:, length:] + sin_cols[:, :length]
    predicted_intensity = lax.optimization_barrier(jnp.sum(field_re * field_re + field_im * field_im, axis=0))
    mode_weight = 1.0 - jnp.sqrt(intensity_measurement.astype(jnp.float32) / jnp.maximum(predicted_intensity, 0.1))
    back_field = jnp.concatenate([mode_weight * field_re, mode_weight * field_im], axis=2).astype(jnp.bfloat16)
    cos_rows = product('jk,mkc->mjc', cosine_lookup, back_field)
    sin_rows = product('jk,mkc->mjc', sine_lookup, back_field)
    fore_re = cos_rows[:, :, :length] + sin_rows[:, :, length:]
    fore_im = cos_rows[:, :, length:] - sin_rows[:, :, :length]
    stacked = jnp.concatenate([fore_re, fore_im], axis=1).astype(jnp.bfloat16)
    cos_cols = product('mjk,kl->mjl', stacked, cosine_lookup)
    sin_cols = product('mjk,kl->mjl', stacked, sine_lookup)
    grad_re = cos_cols[:, :length] + sin_cols[:, length:]
    grad_im = cos_cols[:, length:] - sin_cols[:, :length]
    patch_grad = jnp.concatenate([lax.optimization_barrier(jnp.sum(pupil_re * grad_re + pupil_im * grad_im, axis=0)), lax.optimization_barrier(jnp.sum(pupil_re * grad_im - pupil_im * grad_re, axis=0))], axis=1)
    pupil_term = jnp.concatenate([real_part * grad_re + imag_part * grad_im, real_part * grad_im - imag_part * grad_re], axis=2)
    return (patch_grad, pupil_term)

def add_block(canvas, block, row_start, col_start):
    current = lax.dynamic_slice(canvas, (row_start, col_start), block.shape)
    return lax.dynamic_update_slice(canvas, current + block, (row_start, col_start))

def reference(spectrum, pupils, offsets, measured):
    cosine_lookup, sine_lookup = dft_tables(PATCH)

    def step(number, carry):
        canvas, pupil_sum = carry
        row_start = offsets[number, 0].astype(jnp.int32)
        col_start = offsets[number, 1].astype(jnp.int32)
        patch_real = lax.dynamic_slice(spectrum, (row_start, col_start), (PATCH, PATCH))
        patch_imaginary = lax.dynamic_slice(spectrum, (row_start, col_start + SPEC), (PATCH, PATCH))
        patch_grad, pupil_term = emitter_model(patch_real, patch_imaginary, pupils, measured[number], cosine_lookup, sine_lookup)
        canvas = add_block(canvas, patch_grad[:, :PATCH], row_start, col_start)
        canvas = add_block(canvas, patch_grad[:, PATCH:], row_start, col_start + SPEC)
        return (canvas, pupil_sum + pupil_term)
    start = (jnp.zeros((SPEC, 2 * SPEC), jnp.float32), jnp.zeros((MODES, PATCH, 2 * PATCH), jnp.float32))
    canvas, pupil_sum = lax.fori_loop(0, LEDS, step, start)
    return (canvas.reshape(N_TILE, STRIP, 2 * SPEC), pupil_sum)
```

```python
import math
import jax, jax.numpy as jnp, numpy as np
from jax import lax
from jax.sharding import PartitionSpec as P
from jax.experimental import pallas as pl
from jax.experimental.pallas import tpu as pltpu

f32, bf16 = jnp.float32, jnp.bfloat16


def dft_tables(length):
    positions = np.arange(length, dtype=np.int32)
    angles = (positions[:, None] * positions[None, :] % length).astype(np.float32) * np.float32(
        2.0 * math.pi / length
    )
    factor = np.float32(1.0 / math.sqrt(length))
    return (
        jnp.asarray((np.cos(angles) * factor).astype(bf16)),
        jnp.asarray((np.sin(angles) * factor).astype(bf16)),
    )


def mm(a, b):
    return jnp.dot(a, b, preferred_element_type=f32)


def load_shifted(ref, base, rows, pad):
    start = base // pad * pad
    x = ref[pl.ds(pl.multiple_of(start, pad), rows + pad), :].astype(f32)
    return pltpu.roll(x, rows + pad - (base - start), 0)[:rows]


def build_tables(c_ref, s_ref, fl, fr):
    n = c_ref.shape[0]
    c, s = c_ref[...], s_ref[...]
    fl[:n, :n] = c
    fl[:n, n:] = -s
    fl[n:, :n] = s
    fl[n:, n:] = c
    fr[:n, :n] = c
    fr[:n, n:] = s
    fr[n:, :n] = -s
    fr[n:, n:] = c


def build_permuted(c_ref, s_ref, gl, cb, rpl):
    n = c_ref.shape[0]
    for dst in range(2):
        core = (1 - cb) if dst == 0 else cb

        def body(k, _, dst=dst, core=core):
            row = pl.multiple_of(k * (2 * rpl) + core * rpl, rpl)
            to = pl.multiple_of(dst * (n // 2) + k * rpl, rpl)
            c, s = c_ref[pl.ds(row, rpl), :], s_ref[pl.ds(row, rpl), :]
            gl[pl.ds(to, rpl), :n] = c
            gl[pl.ds(to, rpl), n:] = s
            to = pl.multiple_of(n + dst * (n // 2) + k * rpl, rpl)
            gl[pl.ds(to, rpl), :n] = -s
            gl[pl.ds(to, rpl), n:] = c
            return 0

        lax.fori_loop(0, n // (2 * rpl), body, 0)


def backward_mode(back, hf, gr, gl, fl, pup, patch, pg, term, cb, rpl, first):
    n = hf.shape[0]
    for jb in range(4):
        r = mm(gl[jb * (n // 2):(jb + 1) * (n // 2), :], back[...])
        hf[(jb % 2) * (n // 2):(jb % 2 + 1) * (n // 2), (jb // 2) * n:(jb // 2 + 1) * n] = r.astype(bf16)
    for dst in range(2):
        core = (1 - cb) if dst == 0 else cb
        a = hf[dst * (n // 2):(dst + 1) * (n // 2), :]
        for nb in range(2):
            gr[:, nb * n:(nb + 1) * n] = mm(a, fl[:, nb * n:(nb + 1) * n])

        def body(k, _, dst=dst, core=core):
            row = pl.multiple_of(k * (2 * rpl) + core * rpl, rpl)
            at = pl.multiple_of(k * rpl, rpl)
            g = gr[pl.ds(at, rpl), :]
            g_re, g_im = g[:, :n], g[:, n:]
            p = pup[pl.ds(row, rpl), :].astype(f32)
            p_re, p_im = p[:, :n], p[:, n:]
            q = patch[pl.ds(row, rpl), :].astype(f32)
            q_re, q_im = q[:, :n], q[:, n:]
            term[dst, k, :, :n] = q_re * g_re + q_im * g_im
            term[dst, k, :, n:] = q_re * g_im - q_im * g_re
            a_re = p_re * g_re + p_im * g_im
            a_im = p_re * g_im - p_im * g_re
            if first is True:
                pg[pl.ds(row, rpl), :n] = a_re
                pg[pl.ds(row, rpl), n:] = a_im
            else:
                pg[pl.ds(row, rpl), :n] += a_re
                pg[pl.ds(row, rpl), n:] += a_im
            return 0

        lax.fori_loop(0, n // (2 * rpl), body, 0)


def front_kernel(rpl, half_modes, off, cb_ref, spec_h, pup_h, meas_h, cos_h, sin_h,
                 send_h, keep_h, back_h, patch_h, pg_h,
                 spec, pup, meas, cos, sin, fl, fr, gl, patch, ex, hf, field, back, gr, pg, term, sems, osems):
    modes, n = pup_h.shape[0], pup_h.shape[1]
    spec_len = spec_h.shape[0]
    r, c, cb = off[0], off[1], cb_ref[0]
    rows = n + 16
    start = pl.multiple_of(jnp.minimum(r // 16 * 16, spec_len - rows), 16)
    cp_spec = pltpu.make_async_copy(spec_h.at[pl.ds(start, rows), :], spec.at[pl.ds(0, rows), :], sems.at[0])
    cp_cos = pltpu.make_async_copy(cos_h, cos, sems.at[1])
    cp_sin = pltpu.make_async_copy(sin_h, sin, sems.at[2])
    cp_pup = [pltpu.make_async_copy(pup_h.at[m], pup.at[m], sems.at[4 + m]) for m in range(modes)]
    cp_meas = pltpu.make_async_copy(meas_h, meas, sems.at[3])
    cp_cos.start(); cp_sin.start(); cp_spec.start()
    for m in range(modes):
        cp_pup[m].start()
    cp_meas.start()
    cp_cos.wait(); cp_sin.wait()
    build_tables(cos, sin, fl, fr)
    build_permuted(cos, sin, gl, cb, rpl)
    cp_spec.wait()
    blk = 64
    def take(k, _):
        x = load_shifted(spec, k * blk + (r - start), blk, 16)
        for part in range(2):
            w = pltpu.roll(x[:, part * spec_len:(part + 1) * spec_len], spec_len - c, 1)[:, :n]
            patch[pl.ds(pl.multiple_of(k * blk, blk), blk), part * n:(part + 1) * n] = w.astype(bf16)
        return 0
    lax.fori_loop(0, n // blk, take, 0)
    out_patch = pltpu.make_async_copy(patch, patch_h, osems.at[0])
    out_patch.start()
    for m in range(modes):
        cp_pup[m].wait()

        def exit_rows(k, _, m=m):
            at = pl.multiple_of(k * blk, blk)
            p = pup[m, pl.ds(at, blk), :].astype(f32)
            q = patch[pl.ds(at, blk), :].astype(f32)
            p_re, p_im, q_re, q_im = p[:, :n], p[:, n:], q[:, :n], q[:, n:]
            ex[pl.ds(at, blk), :] = (q_re * p_re - q_im * p_im).astype(bf16)
            ex[pl.ds(pl.multiple_of(n + k * blk, blk), blk), :] = (q_re * p_im + q_im * p_re).astype(bf16)
            return 0
        lax.fori_loop(0, n // blk, exit_rows, 0)
        for jb in range(4):
            v = mm(fl[jb * (n // 2):(jb + 1) * (n // 2), :], ex[...])
            hf[(jb % 2) * (n // 2):(jb % 2 + 1) * (n // 2), (jb // 2) * n:(jb // 2 + 1) * n] = v.astype(bf16)
        for jb in range(2):
            for nb in range(2):
                field[m, jb * (n // 2):(jb + 1) * (n // 2), nb * n:(nb + 1) * n] = mm(
                    hf[jb * (n // 2):(jb + 1) * (n // 2), :], fr[:, nb * n:(nb + 1) * n])
    cp_meas.wait()
    wb = 16

    def weigh(k, _):
        at = pl.multiple_of(k * wb, wb)
        f = [field[m, pl.ds(at, wb), :] for m in range(modes)]
        total = None
        for m in range(modes):
            t = f[m][:, :n] * f[m][:, :n] + f[m][:, n:] * f[m][:, n:]
            total = t if total is None else total + t
        w = 1.0 - jnp.sqrt(meas[pl.ds(at, wb), :].astype(f32) / jnp.maximum(total, 0.1))
        for m in range(modes):
            back[m, pl.ds(at, wb), :] = (w * f[m][:, :n]).astype(bf16)
            back[m, pl.ds(pl.multiple_of(n + k * wb, wb), wb), :] = (w * f[m][:, n:]).astype(bf16)
        return 0
    lax.fori_loop(0, n // wb, weigh, 0)
    out_back = pltpu.make_async_copy(back.at[pl.ds(half_modes, modes - half_modes)], back_h, osems.at[1])
    out_back.start()
    outs = []
    for m in range(half_modes):
        backward_mode(back.at[m], hf, gr, gl, fl, pup.at[m], patch, pg, term.at[m], cb, rpl, m == 0)
        outs += [pltpu.make_async_copy(term.at[m, 0], send_h.at[m], osems.at[3 + 2 * m]),
                 pltpu.make_async_copy(term.at[m, 1], keep_h.at[m], osems.at[4 + 2 * m])]
        outs[-1].start(); outs[-2].start()
    out_pg = pltpu.make_async_copy(pg, pg_h, osems.at[2])
    out_pg.start()
    for o in [out_patch, out_back, out_pg] + outs:
        o.wait()


ANY = pl.BlockSpec(memory_space=pl.ANY)
SM = pl.BlockSpec(memory_space=pltpu.SMEM)


def front(off, cb, spectrum, pupils, measured, cos, sin, led):
    modes, n, _ = pupils.shape
    spec_len = spectrum.shape[0]
    rpl, yx, hm = n // led, led // 2, modes // 2
    sds = jax.ShapeDtypeStruct
    return pl.pallas_call(
        lambda *a: front_kernel(rpl, hm, *a),
        out_shape=(sds((hm, yx, rpl, 2 * n), f32), sds((hm, yx, rpl, 2 * n), f32),
                   sds((modes - hm, 2 * n, n), bf16), sds((n, 2 * n), bf16), sds((n, 2 * n), f32)),
        in_specs=[SM, SM] + [ANY] * 5,
        out_specs=(ANY,) * 5,
        scratch_shapes=[
            pltpu.VMEM((n + 32, 2 * spec_len), bf16), pltpu.VMEM((modes, n, 2 * n), bf16), pltpu.VMEM((n, n), bf16),
            pltpu.VMEM((n, n), bf16), pltpu.VMEM((n, n), bf16),
            pltpu.VMEM((2 * n, 2 * n), bf16), pltpu.VMEM((2 * n, 2 * n), bf16), pltpu.VMEM((2 * n, 2 * n), bf16),
            pltpu.VMEM((n, 2 * n), bf16), pltpu.VMEM((2 * n, n), bf16), pltpu.VMEM((n, 2 * n), bf16),
            pltpu.VMEM((modes, n, 2 * n), f32), pltpu.VMEM((modes, 2 * n, n), bf16),
            pltpu.VMEM((n // 2, 2 * n), f32), pltpu.VMEM((n, 2 * n), f32), pltpu.VMEM((hm, 2, yx, rpl, 2 * n), f32),
            pltpu.SemaphoreType.DMA((4 + modes,)), pltpu.SemaphoreType.DMA((3 + 2 * hm,)),
        ],
        compiler_params=pltpu.CompilerParams(vmem_limit_bytes=56 * 2**20),
        name="front",
    )(off, cb, spectrum, pupils, measured, cos, sin)


def rear_kernel(rpl, strip, off, cb_ref, back_h, patch_h, pg_h, pup_h, cos_h, sin_h,
                send_h, keep_h, ssend_h, skeep_h,
                back, patch, pg, pup, cos, sin, fl, fr, gl, hf, gr, term, rolled, sbuf, sems, osems):
    count, n = pup.shape[0], pup.shape[1]
    modes = pup_h.shape[0]
    r, c, cb = off[0], off[1], cb_ref[0]
    cps = [pltpu.make_async_copy(cos_h, cos, sems.at[0]), pltpu.make_async_copy(sin_h, sin, sems.at[1]),
           pltpu.make_async_copy(back_h, back, sems.at[2]), pltpu.make_async_copy(patch_h, patch, sems.at[3]),
           pltpu.make_async_copy(pup_h.at[pl.ds(modes - count, count)], pup, sems.at[4]),
           pltpu.make_async_copy(pg_h, pg, sems.at[5])]
    for x in cps:
        x.start()
    cps[0].wait(); cps[1].wait()
    build_tables(cos, sin, fl, fr)
    build_permuted(cos, sin, gl, cb, rpl)
    for x in cps[2:]:
        x.wait()
    outs = []
    for m in range(count):
        backward_mode(back.at[m], hf, gr, gl, fl, pup.at[m], patch, pg, term.at[m], cb, rpl, False)
        outs += [pltpu.make_async_copy(term.at[m, 0], send_h.at[m], osems.at[2 + 2 * m]),
                 pltpu.make_async_copy(term.at[m, 1], keep_h.at[m], osems.at[3 + 2 * m])]
        outs[-1].start(); outs[-2].start()
    blk = 64
    rs, cs = lax.rem(r, n), lax.rem(c, n)

    def roll_cols(k, _):
        at = pl.multiple_of(k * blk, blk)
        x = pg[pl.ds(at, blk), :]
        for part in range(2):
            w = pltpu.roll(x[:, part * n:(part + 1) * n], cs, 1)
            rolled[pl.ds(at, blk), part * n:(part + 1) * n] = w

            @pl.when(k == 0)
            def _(w=w, part=part):
                rolled[n:n + blk, part * n:(part + 1) * n] = w
        return 0
    lax.fori_loop(0, n // blk, roll_cols, 0)
    rows = strip // (2 * send_h.shape[1])
    yx = send_h.shape[1]
    for dst in range(2):
        core = (1 - cb) if dst == 0 else cb

        def piece(k, _, dst=dst, core=core):
            h, j = k // yx, lax.rem(k, yx)
            p = h * strip + j * 2 * rows + core * rows
            src = lax.rem(p - rs + n, n)
            x = load_shifted(rolled, src, rows, 8)
            sbuf[dst, 0, j, h] = x[:, :n]
            sbuf[dst, 1, j, h] = x[:, n:]
            return 0
        lax.fori_loop(0, 2 * yx, piece, 0)
    outs += [pltpu.make_async_copy(sbuf.at[0], ssend_h, osems.at[0]), pltpu.make_async_copy(sbuf.at[1], skeep_h, osems.at[1])]
    outs[-1].start(); outs[-2].start()
    for o in outs:
        o.wait()


def rear(off, cb, back, patch, pg, pupils, cos, sin, led, strip):
    n = pupils.shape[1]
    hm = back.shape[0]
    rpl, yx = n // led, led // 2
    rows = strip // led
    sds = jax.ShapeDtypeStruct
    return pl.pallas_call(
        lambda *a: rear_kernel(rpl, strip, *a),
        out_shape=(sds((hm, yx, rpl, 2 * n), f32), sds((hm, yx, rpl, 2 * n), f32),
                   sds((2, yx, 2, rows, n), f32), sds((2, yx, 2, rows, n), f32)),
        in_specs=[SM, SM] + [ANY] * 6,
        out_specs=(ANY,) * 4,
        scratch_shapes=[
            pltpu.VMEM((hm, 2 * n, n), bf16), pltpu.VMEM((n, 2 * n), bf16), pltpu.VMEM((n, 2 * n), f32),
            pltpu.VMEM((hm, n, 2 * n), bf16), pltpu.VMEM((n, n), bf16), pltpu.VMEM((n, n), bf16),
            pltpu.VMEM((2 * n, 2 * n), bf16), pltpu.VMEM((2 * n, 2 * n), bf16), pltpu.VMEM((2 * n, 2 * n), bf16),
            pltpu.VMEM((n, 2 * n), bf16), pltpu.VMEM((n // 2, 2 * n), f32),
            pltpu.VMEM((hm, 2, yx, rpl, 2 * n), f32), pltpu.VMEM((n + 64, 2 * n), f32),
            pltpu.VMEM((2, 2, yx, 2, rows, n), f32),
            pltpu.SemaphoreType.DMA((6,)), pltpu.SemaphoreType.DMA((2 + 2 * hm,)),
        ],
        compiler_params=pltpu.CompilerParams(vmem_limit_bytes=56 * 2**20),
        name="rear",
    )(off, cb, back, patch, pg, pupils, cos, sin)


def bit_of(index, bit):
    return lax.shift_right_logical(index, bit) & 1


def swap(x, axis, bit):
    size = lax.axis_size(axis)
    return lax.ppermute(x, axis, [(i, i ^ (1 << bit)) for i in range(size)])


def pick(x, index, dim):
    return lax.dynamic_index_in_dim(x, index, dim, keepdims=False)


def total(terms):
    out = terms[0]
    for t in terms[1:]:
        out = out + t
    return out


def halve(terms, dims, bit, index):
    at, mine = dims.index(bit), bit_of(index, bit)
    got = swap(total([pick(t, 1 - mine, at) for t in terms]), "led", bit)
    return [pick(t, mine, at) for t in terms] + [got], [b for b in dims if b != bit]


def gather_step(pieces, dims, bit, index):
    at, mine = dims.index(bit), bit_of(index, bit)
    got = swap(jnp.stack([pick(t, 1 - mine, at) for t in pieces]), "led", bit)
    return ([pick(t, mine, at) for t in pieces] + [got[i] for i in range(len(pieces))],
            [b for b in dims if b != bit])


def local(spectrum, pupils, offsets, measured):
    modes, n, _ = pupils.shape
    spec_len = spectrum.shape[0]
    led, tiles = lax.axis_size("led"), lax.axis_size("tile")
    index, z = lax.axis_index("led"), lax.axis_index("tile")
    strip = spec_len // tiles
    nbits = led.bit_length() - 1
    low = [b for b in range(1, 1 + (nbits - 1) // 2)]
    high = [b for b in range(1 + (nbits - 1) // 2, nbits)]
    cube = (2,) * (nbits - 1)
    dims0 = list(range(nbits - 1, 0, -1))
    orders = (low + high, high + low)
    z0, z1 = bit_of(z, 0), bit_of(z, 1)
    cos, sin = dft_tables(n)
    off = offsets[0]
    cb = (index & 1).reshape(1)

    send_a, keep_a, back, patch, pg = front(off, cb, spectrum, pupils, measured[0], cos, sin, led)
    got_a = swap(send_a, "led", 0)
    send_b, keep_b, send_s, keep_s = rear(off, cb, back, patch, pg, pupils, cos, sin, led, strip)
    got_s = swap(send_s, "led", 0)
    got_b = swap(send_b, "led", 0)

    meta = off[None]
    for b in [0] + low + high:
        meta = jnp.concatenate([meta, swap(meta, "led", b)])

    def pupil_plane(keep, got, m):
        terms = [t[m].reshape(cube + t.shape[2:]) for t in (keep, got)]
        dims = dims0
        for b in orders[m % 2]:
            terms, dims = halve(terms, dims, b, index)
        return terms

    def pupil_depth(first, second):
        a, b = total(first), total(second)
        got = swap(jnp.where(z0 == 0, b, a), "tile", 0)
        half = [t.reshape(2, t.shape[0] // 2, t.shape[1]) for t in (jnp.where(z0 == 0, a, b), got)]
        got = swap(total([pick(t, 1 - z1, 0) for t in half]), "tile", 1)
        mine = total([pick(t, z1, 0) for t in half] + [got])
        other = swap(mine, "tile", 1)
        both = jnp.where(z1 == 0, jnp.concatenate([mine, other]), jnp.concatenate([other, mine]))
        far = swap(both, "tile", 0)
        return jnp.where(z0 == 0, jnp.stack([both, far]), jnp.stack([far, both]))

    a_plane = [pupil_plane(keep_a, got_a, m) for m in range(2)]
    out_a = pupil_depth(*a_plane)

    sources = []
    for part in range(2):
        pieces = [t[part].reshape(cube + t.shape[2:]) for t in (keep_s, got_s)]
        ids, dims = [0, 1], dims0
        for b in orders[part]:
            pieces, dims = gather_step(pieces, dims, b, index)
            ids = ids + [i | (1 << b) for i in ids]
        sources.append((ids, pieces))
    rows = strip // led
    column = lax.broadcasted_iota(jnp.int32, (1, 1, n), 2)

    def canvas(h):
        p = h * strip + index * rows + lax.broadcasted_iota(jnp.int32, (2, rows, 1), 1)
        upper = lax.broadcasted_iota(jnp.int32, (2, rows, 1), 0) == 0
        out = []
        for ids, pieces in sources:
            for q in range(2):
                acc = None
                for i, piece in zip(ids, pieces):
                    r, c = meta[i, 0], meta[i, 1]
                    keep = ((p >= r) == upper) & ((column >= c) == (q == 0))
                    t = jnp.where(keep, pick(piece, h, 0)[None], 0.0)
                    acc = t if acc is None else acc + t
                out.append(acc)
        return jnp.concatenate(out, axis=2)

    got = swap(canvas(1 - z0), "tile", 0)
    halfs = [canvas(z0), got]
    got = swap(total([pick(t, 1 - z1, 0) for t in halfs]), "tile", 1)
    spectrum_grad = total([pick(t, z1, 0) for t in halfs] + [got])[None]

    b_plane = [pupil_plane(keep_b, got_b, m) for m in range(2)]
    out_b = pupil_depth(*b_plane)
    return (spectrum_grad, jnp.concatenate([out_a, out_b]))


def solution(mesh):
    return jax.shard_map(
        local,
        mesh=mesh,
        in_specs=(P(), P(), P(("led", "tile"), None), P(("led", "tile"), None, None)),
        out_specs=(P("tile", "led", None), P(None, "led", None)),
        check_vma=False,
    )
```
